128 devices in a mesh: row: 8 (over z, core), col: 16 (over y, x).
Axes of the slice: x: 4, y: 4, z: 4, core: 2. Of those that a mesh axis runs over, the one named last changes fastest.
Arguments:
- inverse: bfloat16 [18432, 18432], P('row', 'col'), may hold values from -0.046875 to 0.046875
- pair_block: bfloat16 [18432, 2560], P('row', 'col'), may hold values from -6 to 6
- coeffs: bfloat16 [5120, 2560], P('row'), may hold values from -0.125 to 0.125
Outputs:
- gradient_ao: bfloat16 [18432, 5120], P('col', 'row')
The draws below stay inside these ranges and needn't reach their ends.
All inputs are finite; a program needn't handle non-finite values.
Results may differ from the reference program's by a relative error of at most 0.0049.
Values may be sent and summed in bfloat16 or wider, within the bound.
A program may use at most 128 MiB of HBM per device.

```python
import jax
import jax.numpy as jnp
from jax import lax

NAUX = 18432
NVIR = 2560
NBAS = 5120


def levels(own_key, dims, cuts, least, top_value):
    gain = 1.0
    for axis_at, parts in cuts:
        draws = jax.random.uniform(jax.random.fold_in(jax.random.fold_in(own_key, 6), axis_at), (parts,), jnp.float32, least / len(cuts), top_value / len(cuts))
        gain = gain * jnp.repeat(jnp.exp(draws), dims[axis_at] // parts).reshape((-1,) + (1,) * (len(dims) - 1 - axis_at))
    return gain


def bell_draw(own_key, dims, scale, limit, shards=(), dtype=jnp.bfloat16):
    factor_of = levels(own_key, dims, shards, -0.22, 0.18) if shards else 1.0
    entries = jax.random.normal(own_key, dims, jnp.float32) * scale * factor_of
    return jnp.minimum(jnp.maximum(entries, -limit), limit).astype(dtype)


def setup_inputs(seed: int = 0) -> dict:
    splits = jax.random.split(jax.random.key(seed), 4)
    return {
        "inverse": bell_draw(splits[0], (NAUX, NAUX), NAUX ** -0.5, 0.046875, ((0, 8), (1, 16))),
        "pair_block": bell_draw(splits[1], (NAUX, NVIR), 1.0, 6.0, ((0, 8), (1, 16))),
        "coeffs": bell_draw(splits[2], (NBAS, NVIR), NVIR ** -0.5, 0.125, ((0, 8),)),
    }


def reference(inverse, pair_block, coeffs):
    product = lax.dot_general(inverse, pair_block, (((0,), (0,)), ((), ())), preferred_element_type=jnp.float32)
    gamma_sum = product - pair_block.astype(jnp.float32)
    gamma_aux = gamma_sum.astype(jnp.bfloat16)
    result = lax.dot_general(gamma_aux, coeffs, (((1,), (1,)), ((), ())), preferred_element_type=jnp.float32)
    return result.astype(jnp.bfloat16)
```

```python
import jax
import jax.numpy as jnp
from jax import lax
from jax.experimental import pallas as pl
from jax.experimental.pallas import tpu as pltpu
from jax.sharding import PartitionSpec as P

MESH = pl.DeviceIdType.MESH
F32, BF16 = jnp.float32, jnp.bfloat16

SLOTS = [
    (0, 0, 0), (1, 0, 0),
    (0, 3, 0), (0, 1, 0), (1, 0, 3), (1, 0, 1),
    (0, 0, 3), (0, 0, 1), (1, 3, 0), (1, 1, 0),
    (0, 2, 0), (1, 0, 2),
    (0, 3, 3), (0, 3, 1), (1, 3, 3), (1, 1, 3),
    (0, 1, 3), (0, 1, 1), (1, 3, 1), (1, 1, 1),
    (0, 0, 2), (1, 2, 0),
    (0, 2, 3), (0, 2, 1), (1, 3, 2), (1, 1, 2),
    (0, 3, 2), (1, 2, 3),
    (0, 1, 2), (1, 2, 1),
    (0, 2, 2), (1, 2, 2),
]
SLOT_OF = {key: at for at, key in enumerate(SLOTS)}


def routes():
    sends, parts = {}, {}

    def add(half, first, second, step_first, step_second, part):
        def key(a, b):
            return (half, a % 4, b % 4) if half == 0 else (half, b % 4, a % 4)

        source = SLOT_OF[key(first, second)]
        target = SLOT_OF[key(first - step_first, second - step_second)]
        step = (step_first, step_second) if half == 0 else (step_second, step_first)
        copy = (source, target, part) + step
        sends.setdefault(source, []).append(copy)
        parts.setdefault(target, []).append(copy)

    for half in (0, 1):
        for step in (1, -1):
            add(half, 0, 0, step, 0, "all")
        add(half, -1, 0, 1, 0, "low")
        add(half, 1, 0, -1, 0, "high")
        for first in (0, -1, 1, 2):
            for step in (1, -1):
                add(half, first, 0, 0, step, "all")
            add(half, first, -1, 0, 1, "low" if first in (0, 1) else "lower")
            add(half, first, 1, 0, -1, "high" if first in (0, 1) else "higher")
    return sends, parts


SENDS, PARTS = routes()
COPIES = sorted({copy for group in SENDS.values() for copy in group}, key=lambda c: (c[1], c[2]))
COPY_ID = {copy: at for at, copy in enumerate(COPIES)}

TICK = 128
LAG2, LAG3, LAG4, LAG5 = 1, 3, 5, 6


def kernel(inv_hbm, pair_hbm, coef_hbm, out_ref, inv, pair, cstage, ct, cts, part, crecv, zsend, keep, zrecv, gamma, acc,
           local, pair_s, pair_r, core_s, core_r, z_s, z_r, ag_s, ag_r, back_s, back_r):
    rows, here = pair_hbm.shape
    cols = inv_hbm.shape[1]
    basis, virt = coef_hbm.shape
    hb = rows // 2
    ticks = virt // TICK
    half_tick, piece = TICK // 2, TICK // 8
    row, col = lax.axis_index("row"), lax.axis_index("col")
    z, core = row // 2, row % 2
    y, x = col // 4, col % 4

    def at_xy(step_x, step_y):
        return (row, (y + step_y) % 4 * 4 + (x + step_x) % 4)

    def at_z(step):
        return ((z + step) % 4 * 2 + core, col)

    sibling = (z * 2 + 1 - core, col)

    def ds(start, size):
        return pl.ds(pl.multiple_of(start, size), size)

    load_pair = pltpu.make_async_copy(pair_hbm, pair.at[pl.ds(0, rows)], local.at[0])
    load_inv = pltpu.make_async_copy(inv_hbm, inv, local.at[1])
    quarter = virt // 4
    load_c = [
        pltpu.make_async_copy(coef_hbm.at[:, pl.ds(k * quarter, quarter)], cstage.at[k % 2], local.at[2 + k]) for k in range(4)
    ]
    load_pair.start()
    load_c[0].start()
    load_c[1].start()
    load_inv.start()

    barrier = pltpu.get_barrier_semaphore()
    for device in (at_xy(1, 0), at_xy(3, 0), at_xy(0, 1), at_xy(0, 3), at_z(1), at_z(2), at_z(3), sibling):
        pl.semaphore_signal(barrier, inc=1, device_id=device, device_id_type=MESH)
    pl.semaphore_wait(barrier, 8)

    def pair_copy(copy):
        source, target, span, step_x, step_y = copy
        start, size = {"all": (0, 80), "low": (0, 48), "high": (48, 32), "lower": (0, 32), "higher": (32, 48)}[span]
        at = COPY_ID[copy]
        return pltpu.make_async_remote_copy(
            pair.at[pl.ds(source * hb + start, size)], pair.at[pl.ds(target * hb + start, size)], pair_s.at[at], pair_r.at[at],
            device_id=at_xy(step_x, step_y), device_id_type=MESH,
        )

    load_pair.wait()
    own = sorted(SENDS[0] + SENDS[1], key=lambda c: (c[3] != 0) != (c[0] == 0))
    for copy in own:
        pair_copy(copy).start()

    acc[...] = jnp.zeros_like(acc)
    for k in range(4):
        load_c[k].wait()
        ct[pl.ds(k * quarter, quarter), :] = cstage[k % 2].T
        if k + 2 < 4:
            load_c[k + 2].start()
    for slot, (half, dx, dy) in enumerate(SLOTS):
        block = (y + dy) % 4 * 4 + (x + dx) % 4
        start = pl.multiple_of(block * rows + half * hb, hb)
        cts[pl.ds(slot * hb, hb), :] = ct[pl.ds(start, hb), :]
    load_inv.wait()

    holds_diag = col // 2 == row
    diag_at = pl.multiple_of(col % 2 * cols, cols)

    def core_copy(u):
        return pltpu.make_async_remote_copy(
            part.at[u % 4, ds((1 - core) * half_tick, half_tick)], crecv.at[ds(u * half_tick, half_tick)],
            core_s.at[u], core_r.at[u], device_id=sibling, device_id_type=MESH,
        )

    def z_copy(u, step):
        return pltpu.make_async_remote_copy(
            zsend.at[ds(u * half_tick + (z + step) % 4 * piece, piece)], zrecv.at[ds((u * 3 + step - 1) * piece, piece)],
            z_s.at[u, step - 1], z_r.at[u, step - 1], device_id=at_z(step), device_id_type=MESH,
        )

    def spread_copy(u, step):
        mine = ds(u * TICK + core * half_tick + z * piece, piece)
        return pltpu.make_async_remote_copy(
            gamma.at[mine], gamma.at[mine], ag_s.at[u, step - 1], ag_r.at[u, step - 1],
            device_id=at_z(step), device_id_type=MESH,
        )

    def back_copy(u):
        mine = ds(u * TICK + core * half_tick, half_tick)
        return pltpu.make_async_remote_copy(
            gamma.at[mine], gamma.at[mine], back_s.at[u], back_r.at[u], device_id=sibling, device_id_type=MESH,
        )

    def product(t):
        for k in range(ticks):
            slots = [s for s in range(2, 32) if s * hb // TICK == k]
            if slots:
                @pl.when(t == k)
                def _():
                    for slot in slots:
                        for copy in PARTS[slot]:
                            pair_copy(copy).wait_recv()
                        for copy in SENDS.get(slot, ()):
                            pair_copy(copy).start()

        @pl.when(t >= 4)
        def _():
            core_copy(t - 4).wait_send()

        now = ds(t * TICK, TICK)
        part[t % 4] = jnp.dot(pair[now, :], inv[...], preferred_element_type=F32)

        @pl.when(holds_diag)
        def _():
            part[t % 4] = part[t % 4] - pair[now, pl.ds(diag_at, cols)].astype(F32)

        core_copy(t).start()

    def add_cores(u):
        core_copy(u).wait_recv()
        total = part[u % 4, ds(core * half_tick, half_tick)] + crecv[ds(u * half_tick, half_tick)]
        zsend[ds(u * half_tick, half_tick)] = total.astype(BF16)
        keep[u % 4] = (
            part[u % 4, ds(core * half_tick + z * piece, piece)] + crecv[ds(u * half_tick + z * piece, piece)]
        )
        for step in (2, 1, 3):
            z_copy(u, step).start()

    def add_z(u):
        for step in (1, 2, 3):
            z_copy(u, step).wait_recv()
        total = keep[u % 4]
        for step in (1, 2, 3):
            total = total + zrecv[ds((u * 3 + step - 1) * piece, piece)].astype(F32)
        gamma[ds(u * TICK + core * half_tick + z * piece, piece)] = total.astype(BF16)
        for step in (2, 1, 3):
            spread_copy(u, step).start()

    def spread_cores(u):
        for step in (1, 2, 3):
            spread_copy(u, step).wait_recv()
        back_copy(u).start()
        for step in (1, 2, 3):
            z_copy(u, step).wait_send()

    def transform(u):
        back_copy(u).wait_recv()
        now = ds(u * TICK, TICK)
        acc[...] += lax.dot_general(gamma[now, :], cts[now, :], (((0,), (0,)), ((), ())), preferred_element_type=F32)
        for step in (1, 2, 3):
            spread_copy(u, step).wait_send()
        back_copy(u).wait_send()

    def tick(t, _):
        for lag, stage in ((LAG2, add_cores), (LAG3, add_z), (LAG4, spread_cores), (0, product), (LAG5, transform)):
            @pl.when((t >= lag) & (t < ticks + lag))
            def _():
                stage(t - lag)
        return 0

    lax.fori_loop(0, ticks + LAG5, tick, 0)
    out_ref[...] = acc[...].astype(BF16)
    for copy in COPIES:
        pair_copy(copy).wait_send()
    for u in range(ticks - 4, ticks):
        core_copy(u).wait_send()


def shards(inverse, pair_block, coeffs):
    here, cols = inverse.shape
    rows = pair_block.shape[1]
    basis, virt = coeffs.shape
    ticks = virt // TICK
    dma = pltpu.SemaphoreType.DMA
    any_space = pl.BlockSpec(memory_space=pl.ANY)
    return pl.pallas_call(
        kernel,
        out_shape=jax.ShapeDtypeStruct((cols, basis), BF16),
        in_specs=[any_space] * 3,
        out_specs=pl.BlockSpec(memory_space=pltpu.VMEM),
        scratch_shapes=[
            pltpu.VMEM((here, cols), BF16),
            pltpu.VMEM((virt, here), BF16),
            pltpu.VMEM((2, basis, virt // 4), BF16),
            pltpu.VMEM((virt, basis), BF16),
            pltpu.VMEM((virt, basis), BF16),
            pltpu.VMEM((4, TICK, cols), F32),
            pltpu.VMEM((virt // 2, cols), F32),
            pltpu.VMEM((virt // 2, cols), BF16),
            pltpu.VMEM((4, TICK // 8, cols), F32),
            pltpu.VMEM((ticks * 3 * TICK // 8, cols), BF16),
            pltpu.VMEM((virt, cols), BF16),
            pltpu.VMEM((cols, basis), F32),
            dma((6,)),
            dma((len(COPIES),)), dma((len(COPIES),)),
            dma((ticks,)), dma((ticks,)),
            dma((ticks, 3)), dma((ticks, 3)),
            dma((ticks, 3)), dma((ticks, 3)),
            dma((ticks,)), dma((ticks,)),
        ],
        compiler_params=pltpu.CompilerParams(collective_id=0, has_side_effects=True, vmem_limit_bytes=60 << 20),
    )(inverse, pair_block.T, coeffs)


def solution(mesh):
    placed = (P("row", "col"), P("row", "col"), P("row", None))
    return jax.shard_map(
        shards, mesh=mesh, in_specs=placed, out_specs=P("col", "row"), check_vma=False
    )
```

```python
import jax
import jax.numpy as jnp
from jax import lax
from jax.experimental import pallas as pl
from jax.experimental.pallas import tpu as pltpu
from jax.sharding import PartitionSpec as P

MESH = pl.DeviceIdType.MESH
F32, BF16 = jnp.float32, jnp.bfloat16

PARTS = ((0, 48), (48, 32))
HALF = 80
ARRIVALS = [
    (True, [(0, 3, 0), (0, 1, 0), (1, 0, 3), (1, 0, 1)]),
    (True, [(0, 0, 3), (0, 0, 1), (1, 3, 0), (1, 1, 0)]),
    (False, [(0, 2, 0), (1, 0, 2)]),
    (True, [(0, 3, 3), (0, 3, 1), (1, 3, 3), (1, 1, 3)]),
    (True, [(0, 1, 3), (0, 1, 1), (1, 3, 1), (1, 1, 1)]),
    (False, [(0, 0, 2), (1, 2, 0)]),
    (True, [(0, 2, 3), (0, 2, 1), (1, 3, 2), (1, 1, 2)]),
    (False, [(0, 3, 2), (1, 2, 3)]),
    (False, [(0, 1, 2), (1, 2, 1)]),
    (False, [(0, 2, 2), (1, 2, 2)]),
]


def slots():
    order = [(half, 0, 0, part) for half in (0, 1) for part in (0, 1)]
    groups = []
    for whole, blocks in ARRIVALS:
        for parts in ((0,), (1,)) if whole else ((0, 1),):
            first = len(order)
            order += [block + (part,) for part in parts for block in blocks]
            groups.append(range(first, len(order)))
    return order, groups


SLOTS, GROUPS = slots()
SLOT_OF = {key: at for at, key in enumerate(SLOTS)}
SIZES = [PARTS[key[3]][1] for key in SLOTS]
STARTS = [sum(SIZES[:at]) for at in range(len(SIZES))]


def routes():
    sends, filled = {}, {}

    def add(half, first, second, step_first, step_second, parts):
        def key(a, b, part):
            return (half, a % 4, b % 4, part) if half == 0 else (half, b % 4, a % 4, part)

        step = (step_first, step_second) if half == 0 else (step_second, step_first)
        for part in parts:
            source = SLOT_OF[key(first, second, part)]
            target = SLOT_OF[key(first - step_first, second - step_second, part)]
            copy = (source, target) + step
            sends.setdefault(source, []).append(copy)
            filled[target] = copy

    for half in (0, 1):
        for step in (1, -1):
            add(half, 0, 0, step, 0, (0, 1))
        add(half, -1, 0, 1, 0, (0,))
        add(half, 1, 0, -1, 0, (1,))
        for first in (0, -1, 1, 2):
            for step in (1, -1):
                add(half, first, 0, 0, step, (0, 1))
            part = 0 if first in (0, 1) else 1
            add(half, first, -1, 0, 1, (part,))
            add(half, first, 1, 0, -1, (1 - part,))
    return sends, filled


SENDS, FILLED = routes()
COPIES = [FILLED[slot] for slot in sorted(FILLED)]

TICK = 128
DIRECT = 4
RELAY_LAGS = (1, 2.5, 4, 5.5, 7, 7.5)
DIRECT_LAGS = (1, None, 2.5, None, 4, 4.5)


def kernel(inv_hbm, pair_hbm, coef_hbm, out_ref, inv, pair, cstage, ct, cts, part, crecv, zsend, keep, zrecv, gamma, acc,
           local, pair_s, pair_r, core_s, core_r, z_s, z_r, ag_s, ag_r, back_s, back_r):
    rows, here = pair_hbm.shape
    cols = inv_hbm.shape[1]
    basis, virt = coef_hbm.shape
    ticks = virt // TICK
    half_tick, piece = TICK // 2, TICK // 8
    row, col = lax.axis_index("row"), lax.axis_index("col")
    z, core = row // 2, row % 2
    y, x = col // 4, col % 4

    def at_xy(step_x, step_y):
        return (row, (y + step_y) % 4 * 4 + (x + step_x) % 4)

    def at_z(step):
        return ((z + step) % 4 * 2 + core, col)

    sibling = (z * 2 + 1 - core, col)

    def ds(start, size):
        return pl.ds(pl.multiple_of(start, size), size)

    load_pair = pltpu.make_async_copy(pair_hbm, pair.at[pl.ds(0, rows)], local.at[0])
    load_inv = pltpu.make_async_copy(inv_hbm, inv, local.at[1])
    quarter = virt // 4
    load_c = [
        pltpu.make_async_copy(coef_hbm.at[:, pl.ds(k * quarter, quarter)], cstage.at[k % 2], local.at[2 + k]) for k in range(4)
    ]
    load_pair.start()
    load_c[0].start()
    load_c[1].start()
    load_inv.start()

    barrier = pltpu.get_barrier_semaphore()
    for device in (at_xy(1, 0), at_xy(3, 0), at_xy(0, 1), at_xy(0, 3), at_z(1), at_z(2), at_z(3), sibling):
        pl.semaphore_signal(barrier, inc=1, device_id=device, device_id_type=MESH)
    pl.semaphore_wait(barrier, 8)

    def pair_copy(copy):
        source, target, step_x, step_y = copy
        origin = pair_hbm if source < 4 else pair
        size, at = SIZES[source], COPIES.index(copy)
        return pltpu.make_async_remote_copy(
            origin.at[pl.ds(STARTS[source], size)], pair.at[pl.ds(STARTS[target], size)], pair_s.at[at], pair_r.at[at],
            device_id=at_xy(step_x, step_y), device_id_type=MESH,
        )

    own = [copy for slot in range(4) for copy in SENDS[slot]]
    for copy in sorted(own, key=lambda c: ((c[2] != 0) != (c[0] < 2), c[0] % 2)):
        pair_copy(copy).start()

    acc[...] = jnp.zeros_like(acc)
    for k in range(4):
        load_c[k].wait()
        ct[pl.ds(k * quarter, quarter), :] = cstage[k % 2].T
        if k + 2 < 4:
            load_c[k + 2].start()
    for slot, (half, dx, dy, part_of) in enumerate(SLOTS):
        block = (y + dy) % 4 * 4 + (x + dx) % 4
        start = pl.multiple_of(block * rows + half * HALF + PARTS[part_of][0], 16)
        cts[pl.ds(STARTS[slot], SIZES[slot]), :] = ct[pl.ds(start, SIZES[slot]), :]
    load_pair.wait()
    load_inv.wait()

    holds_diag = col // 2 == row
    diag_at = pl.multiple_of(col % 2 * cols, cols)

    def core_copy(u):
        return pltpu.make_async_remote_copy(
            part.at[u % 4, ds((1 - core) * half_tick, half_tick)], crecv.at[ds(u * half_tick, half_tick)],
            core_s.at[u], core_r.at[u], device_id=sibling, device_id_type=MESH,
        )

    ahead = 1 - 2 * core
    steps = (ahead, -ahead, ahead)

    def piece_at(u, step):
        return ds(u * half_tick + (z + step + 4) % 4 * piece, piece)

    def z_send(u, k, step, owner):
        return pltpu.make_async_remote_copy(
            zsend.at[piece_at(u, owner)], zrecv.at[ds((u * 3 + k) * piece, piece)],
            z_s.at[u, k], z_r.at[u, k], device_id=at_z(step + 4), device_id_type=MESH,
        )

    def spread_send(u, k, step, owner):
        rows_of = ds(u * TICK + core * half_tick + (z + owner + 4) % 4 * piece, piece)
        return pltpu.make_async_remote_copy(
            gamma.at[rows_of], gamma.at[rows_of], ag_s.at[u, k], ag_r.at[u, k],
            device_id=at_z(step + 4), device_id_type=MESH,
        )

    def back_copy(u):
        mine = ds(u * TICK + core * half_tick, half_tick)
        return pltpu.make_async_remote_copy(
            gamma.at[mine], gamma.at[mine], back_s.at[u], back_r.at[u], device_id=sibling, device_id_type=MESH,
        )

    def arrive(t):
        for group in GROUPS:
            @pl.when(t == STARTS[group[0]] // TICK)
            def _():
                for slot in group:
                    pair_copy(FILLED[slot]).wait_recv()
                    for copy in SENDS.get(slot, ()):
                        pair_copy(copy).start()

    def product(t):
        @pl.when(t >= 4)
        def _():
            core_copy(t - 4).wait_send()

        now = ds(t * TICK, TICK)
        part[t % 4] = jnp.dot(pair[now, :], inv[...], preferred_element_type=F32)

        @pl.when(holds_diag)
        def _():
            part[t % 4] = part[t % 4] - pair[now, pl.ds(diag_at, cols)].astype(F32)

        core_copy(t).start()

    def add_cores(u, direct):
        core_copy(u).wait_recv()
        total = part[u % 4, ds(core * half_tick, half_tick)] + crecv[ds(u * half_tick, half_tick)]
        zsend[ds(u * half_tick, half_tick)] = total.astype(BF16)
        z_send(u, 0, 2 if direct else ahead, 2).start()
        z_send(u, 1, -ahead, -ahead).start()
        if direct:
            z_send(u, 2, ahead, ahead).start()
        for k, owner in enumerate((0,) if direct else (0, ahead)):
            at = (z + owner + 4) % 4 * piece
            keep[u % 8, pl.ds(k * piece, piece)] = (
                part[u % 4, ds(core * half_tick + at, piece)] + crecv[ds(u * half_tick + at, piece)]
            )

    def relay(u, direct):
        z_send(u, 0, ahead, 2).wait_recv()
        total = keep[u % 8, pl.ds(piece, piece)] + zrecv[ds(u * 3 * piece, piece)].astype(F32)
        zsend[piece_at(u, ahead)] = total.astype(BF16)
        z_send(u, 2, ahead, ahead).start()

    def add_z(u, direct):
        total = keep[u % 8, pl.ds(0, piece)]
        for k in (1, 2, 0) if direct else (1, 2):
            z_send(u, k, steps[k], 0).wait_recv()
            total = total + zrecv[ds((u * 3 + k) * piece, piece)].astype(F32)
        gamma[ds(u * TICK + core * half_tick + z * piece, piece)] = total.astype(BF16)
        if direct:
            spread_send(u, 2, 2, 0).start()
        spread_send(u, 0, ahead, 0).start()
        spread_send(u, 1, -ahead, 0).start()

    def spread_relay(u, direct):
        spread_send(u, 0, ahead, -ahead).wait_recv()
        spread_send(u, 2, ahead, -ahead).start()

    def spread_cores(u, direct):
        if direct:
            spread_send(u, 0, ahead, -ahead).wait_recv()
        spread_send(u, 1, -ahead, ahead).wait_recv()
        spread_send(u, 2, ahead, 2).wait_recv()
        back_copy(u).start()

    def transform(u, direct):
        back_copy(u).wait_recv()

        @pl.when(u % 2 == 1)
        def _():
            now = ds((u - 1) * TICK, 2 * TICK)
            acc[...] += lax.dot_general(gamma[now, :], cts[now, :], (((0,), (0,)), ((), ())), preferred_element_type=F32)

        for k in range(3):
            z_send(u, k, steps[k], 0).wait_send()
            spread_send(u, k, steps[k], 0).wait_send()
        back_copy(u).wait_send()

    stages = (add_cores, relay, add_z, spread_relay, spread_cores, transform)
    turn = ticks - DIRECT
    plan = [(lag, 0, turn, stage, False) for lag, stage in zip(RELAY_LAGS, stages) if turn and lag is not None]
    plan += [(lag, turn, ticks, stage, True) for lag, stage in zip(DIRECT_LAGS, stages) if DIRECT and lag is not None]

    def tick(t, _):
        def run(after):
            for lag, first, last, stage, direct in plan:
                if (lag != int(lag)) == after:
                    @pl.when((t >= int(lag) + first) & (t < int(lag) + last))
                    def _():
                        stage(t - int(lag), direct)

        @pl.when(t < ticks)
        def _():
            arrive(t)

        run(False)

        @pl.when(t < ticks)
        def _():
            product(t)

        run(True)
        return 0

    lax.fori_loop(0, max(int(lag) + last for lag, _, last, _, _ in plan), tick, 0)
    out_ref[...] = acc[...].astype(BF16)
    for copy in COPIES:
        pair_copy(copy).wait_send()
    for u in range(ticks - 4, ticks):
        core_copy(u).wait_send()


def shards(inverse, pair_block, coeffs):
    here, cols = inverse.shape
    rows = pair_block.shape[1]
    basis, virt = coeffs.shape
    ticks = virt // TICK
    dma = pltpu.SemaphoreType.DMA
    any_space = pl.BlockSpec(memory_space=pl.ANY)
    return pl.pallas_call(
        kernel,
        out_shape=jax.ShapeDtypeStruct((cols, basis), BF16),
        in_specs=[any_space] * 3,
        out_specs=pl.BlockSpec(memory_space=pltpu.VMEM),
        scratch_shapes=[
            pltpu.VMEM((here, cols), BF16),
            pltpu.VMEM((virt, here), BF16),
            pltpu.VMEM((2, basis, virt // 4), BF16),
            pltpu.VMEM((virt, basis), BF16),
            pltpu.VMEM((virt, basis), BF16),
            pltpu.VMEM((4, TICK, cols), F32),
            pltpu.VMEM((virt // 2, cols), F32),
            pltpu.VMEM((virt // 2, cols), BF16),
            pltpu.VMEM((8, TICK // 4, cols), F32),
            pltpu.VMEM((ticks * 3 * TICK // 8, cols), BF16),
            pltpu.VMEM((virt, cols), BF16),
            pltpu.VMEM((cols, basis), F32),
            dma((6,)),
            dma((len(COPIES),)), dma((len(COPIES),)),
            dma((ticks,)), dma((ticks,)),
            dma((ticks, 3)), dma((ticks, 3)),
            dma((ticks, 3)), dma((ticks, 3)),
            dma((ticks,)), dma((ticks,)),
        ],
        compiler_params=pltpu.CompilerParams(collective_id=0, has_side_effects=True, vmem_limit_bytes=51 << 20),
    )(inverse, pair_block.T, coeffs)


def solution(mesh):
    placed = (P("row", "col"), P("row", "col"), P("row", None))
    return jax.shard_map(
        shards, mesh=mesh, in_specs=placed, out_specs=P("col", "row"), check_vma=False
    )
```

```python
import jax
import jax.numpy as jnp
from jax import lax
from jax.experimental import pallas as pl
from jax.experimental.pallas import tpu as pltpu
from jax.sharding import PartitionSpec as P

MESH = pl.DeviceIdType.MESH
F32, BF16 = jnp.float32, jnp.bfloat16

PARTS = ((0, 48), (48, 32))
HALF = 80
ARRIVALS = [
    (True, [(0, 3, 0), (0, 1, 0), (1, 0, 3), (1, 0, 1)]),
    (True, [(0, 0, 3), (0, 0, 1), (1, 3, 0), (1, 1, 0)]),
    (False, [(0, 2, 0), (1, 0, 2)]),
    (True, [(0, 3, 3), (0, 3, 1), (1, 3, 3), (1, 1, 3)]),
    (True, [(0, 1, 3), (0, 1, 1), (1, 3, 1), (1, 1, 1)]),
    (False, [(0, 0, 2), (1, 2, 0)]),
    (True, [(0, 2, 3), (0, 2, 1), (1, 3, 2), (1, 1, 2)]),
    (False, [(0, 3, 2), (1, 2, 3)]),
    (False, [(0, 1, 2), (1, 2, 1)]),
    (False, [(0, 2, 2), (1, 2, 2)]),
]


def slots():
    order = [(half, 0, 0, part) for half in (0, 1) for part in (0, 1)]
    groups = []
    for whole, blocks in ARRIVALS:
        for parts in ((0,), (1,)) if whole else ((0, 1),):
            first = len(order)
            order += [block + (part,) for part in parts for block in blocks]
            groups.append(range(first, len(order)))
    return order, groups


SLOTS, GROUPS = slots()
SLOT_OF = {key: at for at, key in enumerate(SLOTS)}
SIZES = [PARTS[key[3]][1] for key in SLOTS]
STARTS = [sum(SIZES[:at]) for at in range(len(SIZES))]


def routes():
    sends, filled = {}, {}

    def add(half, first, second, step_first, step_second, parts):
        def key(a, b, part):
            return (half, a % 4, b % 4, part) if half == 0 else (half, b % 4, a % 4, part)

        step = (step_first, step_second) if half == 0 else (step_second, step_first)
        for part in parts:
            source = SLOT_OF[key(first, second, part)]
            target = SLOT_OF[key(first - step_first, second - step_second, part)]
            copy = (source, target) + step
            sends.setdefault(source, []).append(copy)
            filled[target] = copy

    for half in (0, 1):
        for step in (1, -1):
            add(half, 0, 0, step, 0, (0, 1))
        add(half, -1, 0, 1, 0, (0,))
        add(half, 1, 0, -1, 0, (1,))
        for first in (0, -1, 1, 2):
            for step in (1, -1):
                add(half, first, 0, 0, step, (0, 1))
            part = 0 if first in (0, 1) else 1
            add(half, first, -1, 0, 1, (part,))
            add(half, first, 1, 0, -1, (1 - part,))
    return sends, filled


SENDS, FILLED = routes()
COPIES = [FILLED[slot] for slot in sorted(FILLED)]

TICK = 128
DIRECT = 2
RELAY_LAGS = (1, 2.5, 4, 5.5, 7, 7.5)
DIRECT_LAGS = (1, None, 2.5, None, 4, 4.5)


def kernel(inv_hbm, pair_hbm, coef_hbm, out_ref, inv, pair, cstage, ct, cts, part, crecv, zsend, keep, zrecv, gamma, acc,
           local, pair_s, pair_r, core_s, core_r, z_s, z_r, ag_s, ag_r, back_s, back_r):
    rows, here = pair_hbm.shape
    cols = inv_hbm.shape[1]
    basis, virt = coef_hbm.shape
    ticks = virt // TICK
    half_tick, piece = TICK // 2, TICK // 8
    row, col = lax.axis_index("row"), lax.axis_index("col")
    z, core = row // 2, row % 2
    y, x = col // 4, col % 4

    def at_xy(step_x, step_y):
        return (row, (y + step_y) % 4 * 4 + (x + step_x) % 4)

    def at_z(step):
        return ((z + step) % 4 * 2 + core, col)

    sibling = (z * 2 + 1 - core, col)

    def ds(start, size):
        return pl.ds(pl.multiple_of(start, size), size)

    load_pair = pltpu.make_async_copy(pair_hbm, pair.at[pl.ds(0, rows)], local.at[0])
    load_inv = pltpu.make_async_copy(inv_hbm, inv, local.at[1])
    quarter = virt // 4
    load_c = [
        pltpu.make_async_copy(coef_hbm.at[:, pl.ds(k * quarter, quarter)], cstage.at[k % 2], local.at[2 + k]) for k in range(4)
    ]
    load_pair.start()
    load_c[0].start()
    load_c[1].start()
    load_inv.start()

    barrier = pltpu.get_barrier_semaphore()
    for device in (at_xy(1, 0), at_xy(3, 0), at_xy(0, 1), at_xy(0, 3), at_z(1), at_z(2), at_z(3), sibling):
        pl.semaphore_signal(barrier, inc=1, device_id=device, device_id_type=MESH)
    pl.semaphore_wait(barrier, 8)

    def pair_copy(copy):
        source, target, step_x, step_y = copy
        origin = pair_hbm if source < 4 else pair
        size, at = SIZES[source], COPIES.index(copy)
        return pltpu.make_async_remote_copy(
            origin.at[pl.ds(STARTS[source], size)], pair.at[pl.ds(STARTS[target], size)], pair_s.at[at], pair_r.at[at],
            device_id=at_xy(step_x, step_y), device_id_type=MESH,
        )

    own = [copy for slot in range(4) for copy in SENDS[slot]]
    for copy in sorted(own, key=lambda c: ((c[2] != 0) != (c[0] < 2), c[0] % 2)):
        pair_copy(copy).start()

    acc[...] = jnp.zeros_like(acc)
    for k in range(4):
        load_c[k].wait()
        ct[pl.ds(k * quarter, quarter), :] = cstage[k % 2].T
        if k + 2 < 4:
            load_c[k + 2].start()
    for slot, (half, dx, dy, part_of) in enumerate(SLOTS):
        block = (y + dy) % 4 * 4 + (x + dx) % 4
        start = pl.multiple_of(block * rows + half * HALF + PARTS[part_of][0], 16)
        cts[pl.ds(STARTS[slot], SIZES[slot]), :] = ct[pl.ds(start, SIZES[slot]), :]
    load_pair.wait()
    load_inv.wait()

    holds_diag = col // 2 == row
    diag_at = pl.multiple_of(col % 2 * cols, cols)

    def core_copy(u):
        return pltpu.make_async_remote_copy(
            part.at[u % 4, ds((1 - core) * half_tick, half_tick)], crecv.at[ds(u * half_tick, half_tick)],
            core_s.at[u], core_r.at[u], device_id=sibling, device_id_type=MESH,
        )

    ahead = 1 - 2 * core
    steps = (ahead, -ahead, ahead)

    def piece_at(u, step):
        return ds(u * half_tick + (z + step + 4) % 4 * piece, piece)

    def z_send(u, k, step, owner):
        return pltpu.make_async_remote_copy(
            zsend.at[piece_at(u, owner)], zrecv.at[ds((u * 3 + k) * piece, piece)],
            z_s.at[u, k], z_r.at[u, k], device_id=at_z(step + 4), device_id_type=MESH,
        )

    def spread_send(u, k, step, owner):
        rows_of = ds(u * TICK + core * half_tick + (z + owner + 4) % 4 * piece, piece)
        return pltpu.make_async_remote_copy(
            gamma.at[rows_of], gamma.at[rows_of], ag_s.at[u, k], ag_r.at[u, k],
            device_id=at_z(step + 4), device_id_type=MESH,
        )

    def back_copy(u):
        mine = ds(u * TICK + core * half_tick, half_tick)
        return pltpu.make_async_remote_copy(
            gamma.at[mine], gamma.at[mine], back_s.at[u], back_r.at[u], device_id=sibling, device_id_type=MESH,
        )

    def arrive(t):
        for group in GROUPS:
            @pl.when(t == STARTS[group[0]] // TICK)
            def _():
                for slot in group:
                    pair_copy(FILLED[slot]).wait_recv()
                    for copy in SENDS.get(slot, ()):
                        pair_copy(copy).start()

    def product(t):
        @pl.when(t >= 4)
        def _():
            core_copy(t - 4).wait_send()

        now = ds(t * TICK, TICK)
        part[t % 4] = jnp.dot(pair[now, :], inv[...], preferred_element_type=F32)

        @pl.when(holds_diag)
        def _():
            part[t % 4] = part[t % 4] - pair[now, pl.ds(diag_at, cols)].astype(F32)

        core_copy(t).start()

    def add_cores(u, direct):
        core_copy(u).wait_recv()
        total = part[u % 4, ds(core * half_tick, half_tick)] + crecv[ds(u * half_tick, half_tick)]
        zsend[ds(u * half_tick, half_tick)] = total.astype(BF16)
        z_send(u, 0, 2 if direct else ahead, 2).start()
        z_send(u, 1, -ahead, -ahead).start()
        if direct:
            z_send(u, 2, ahead, ahead).start()
        for k, owner in enumerate((0,) if direct else (0, ahead)):
            at = (z + owner + 4) % 4 * piece
            keep[u % 8, pl.ds(k * piece, piece)] = (
                part[u % 4, ds(core * half_tick + at, piece)] + crecv[ds(u * half_tick + at, piece)]
            )

    def relay(u, direct):
        z_send(u, 0, ahead, 2).wait_recv()
        total = keep[u % 8, pl.ds(piece, piece)] + zrecv[ds(u * 3 * piece, piece)].astype(F32)
        zsend[piece_at(u, ahead)] = total.astype(BF16)
        z_send(u, 2, ahead, ahead).start()

    def add_z(u, direct):
        total = keep[u % 8, pl.ds(0, piece)]
        for k in (1, 2, 0) if direct else (1, 2):
            z_send(u, k, steps[k], 0).wait_recv()
            total = total + zrecv[ds((u * 3 + k) * piece, piece)].astype(F32)
        gamma[ds(u * TICK + core * half_tick + z * piece, piece)] = total.astype(BF16)
        if direct:
            spread_send(u, 2, 2, 0).start()
        spread_send(u, 0, ahead, 0).start()
        spread_send(u, 1, -ahead, 0).start()

    def spread_relay(u, direct):
        spread_send(u, 0, ahead, -ahead).wait_recv()
        spread_send(u, 2, ahead, -ahead).start()

    def spread_cores(u, direct):
        if direct:
            spread_send(u, 0, ahead, -ahead).wait_recv()
        spread_send(u, 1, -ahead, ahead).wait_recv()
        spread_send(u, 2, ahead, 2).wait_recv()
        back_copy(u).start()

    def transform(u, direct):
        back_copy(u).wait_recv()

        @pl.when(u % 2 == 1)
        def _():
            now = ds((u - 1) * TICK, 2 * TICK)
            acc[...] += lax.dot_general(gamma[now, :], cts[now, :], (((0,), (0,)), ((), ())), preferred_element_type=F32)

        for k in range(3):
            z_send(u, k, steps[k], 0).wait_send()
            spread_send(u, k, steps[k], 0).wait_send()
        back_copy(u).wait_send()

    stages = (add_cores, relay, add_z, spread_relay, spread_cores, transform)
    turn = ticks - DIRECT
    plan = [(lag, 0, turn, stage, False) for lag, stage in zip(RELAY_LAGS, stages) if turn and lag is not None]
    plan += [(lag, turn, ticks, stage, True) for lag, stage in zip(DIRECT_LAGS, stages) if DIRECT and lag is not None]

    def tick(t, _):
        def run(after):
            for lag, first, last, stage, direct in plan:
                if (lag != int(lag)) == after:
                    @pl.when((t >= int(lag) + first) & (t < int(lag) + last))
                    def _():
                        stage(t - int(lag), direct)

        @pl.when(t < ticks)
        def _():
            arrive(t)

        run(False)

        @pl.when(t < ticks)
        def _():
            product(t)

        run(True)
        return 0

    lax.fori_loop(0, max(int(lag) + last for lag, _, last, _, _ in plan), tick, 0)
    out_ref[...] = acc[...].astype(BF16)
    for copy in COPIES:
        pair_copy(copy).wait_send()
    for u in range(ticks - 4, ticks):
        core_copy(u).wait_send()


def shards(inverse, pair_block, coeffs):
    here, cols = inverse.shape
    rows = pair_block.shape[1]
    basis, virt = coeffs.shape
    ticks = virt // TICK
    dma = pltpu.SemaphoreType.DMA
    any_space = pl.BlockSpec(memory_space=pl.ANY)
    return pl.pallas_call(
        kernel,
        out_shape=jax.ShapeDtypeStruct((cols, basis), BF16),
        in_specs=[any_space] * 3,
        out_specs=pl.BlockSpec(memory_space=pltpu.VMEM),
        scratch_shapes=[
            pltpu.VMEM((here, cols), BF16),
            pltpu.VMEM((virt, here), BF16),
            pltpu.VMEM((2, basis, virt // 4), BF16),
            pltpu.VMEM((virt, basis), BF16),
            pltpu.VMEM((virt, basis), BF16),
            pltpu.VMEM((4, TICK, cols), F32),
            pltpu.VMEM((virt // 2, cols), F32),
            pltpu.VMEM((virt // 2, cols), BF16),
            pltpu.VMEM((8, TICK // 4, cols), F32),
            pltpu.VMEM((ticks * 3 * TICK // 8, cols), BF16),
            pltpu.VMEM((virt, cols), BF16),
            pltpu.VMEM((cols, basis), F32),
            dma((6,)),
            dma((len(COPIES),)), dma((len(COPIES),)),
            dma((ticks,)), dma((ticks,)),
            dma((ticks, 3)), dma((ticks, 3)),
            dma((ticks, 3)), dma((ticks, 3)),
            dma((ticks,)), dma((ticks,)),
        ],
        compiler_params=pltpu.CompilerParams(collective_id=0, has_side_effects=True, vmem_limit_bytes=51 << 20),
    )(inverse, pair_block.T, coeffs)


def solution(mesh):
    placed = (P("row", "col"), P("row", "col"), P("row", None))
    return jax.shard_map(
        shards, mesh=mesh, in_specs=placed, out_specs=P("col", "row"), check_vma=False
    )
```
